32 devices in a mesh: layer: 8 (over y, x, core), dp: 4 (over z).
Axes of the slice: x: 2, y: 2, z: 4, core: 2. Of those that a mesh axis runs over, the one named last changes fastest.
Arguments:
- activations: bfloat16 [8, 1024, 2048], P('layer', 'dp')
- factor_old: float32 [8, 2048, 2048], P('layer', 'dp'), as said below
- cross_old: float32 [8, 2048, 2048], P('layer', 'dp')
- gradients: bfloat16 [8, 2048, 1024], P('layer', 'dp'), may hold values from -6 to 6
- moments: bfloat16 [8, 2048, 1024], P('layer', 'dp'), may hold values from -6 to 6
- exponents: int32 [8, 16], P('layer', 'dp'), may hold values from -3 to 2
- master: float32 [8, 2048, 1024], P('layer', 'dp'), may hold values from -6 to 6
Outputs:
- factor_new: float32 [8, 2048, 2048], P('layer', 'dp')
- cross_new: float32 [8, 2048, 2048], P('layer', 'dp')
- moments_new: bfloat16 [8, 2048, 1024], P('layer', 'dp')
- master_new: float32 [8, 2048, 1024], P('layer', 'dp')
- replicas: bfloat16 [8, 2048, 1024], P('layer')
The draws below stay inside these ranges and needn't reach their ends.
Inputs may be any that keep to these rules, and one draw needn't show every extreme that they name: factor_old is symmetric in its last two dimensions, and its diagonal entries lie between 0.6 and 1.4.
All inputs are finite; a program needn't handle non-finite values.
Results may differ from the reference program's by a relative error of at most 0.0025.
Values may be sent and summed in bfloat16 or wider, within the bound.
A program may use at most 128 MiB of HBM per device.

```python
import jax
import jax.numpy as jnp
from jax import lax

FEATURES = 2048
OUTPUTS = 1024
SCALE_BLOCK = 128
LAYERS = 8
TOKENS = 1024


def draw_activations(key, part):
    subkeys = jax.random.split(jax.random.fold_in(key, 101), 2)
    persist = jax.random.uniform(subkeys[0], (FEATURES,), jnp.float32, 0.3, 0.95)
    noise = jax.random.normal(subkeys[1], (LAYERS, TOKENS, FEATURES), jnp.float32)
    renewal = jnp.sqrt(1.0 - persist * persist)

    def advance(previous, layer_noise):
        following = persist * previous + renewal * layer_noise
        return (following, following)
    _, stacked = lax.scan(advance, noise[0], noise[1:])
    result = jnp.concatenate([noise[0][None], stacked], 0)
    return result.astype(jnp.bfloat16)


def draw_factor_old(key, part):
    subkeys = jax.random.split(jax.random.fold_in(key, 202), 2)
    diagonal_values = jax.random.uniform(subkeys[0], (LAYERS, FEATURES), jnp.float32, 0.6, 1.4)
    raw = jax.random.normal(subkeys[1], (LAYERS, FEATURES, FEATURES), jnp.float32)
    raw = raw * (0.3 / jnp.sqrt(jnp.float32(FEATURES)))
    symmetric = (raw + jnp.swapaxes(raw, 1, 2)) * 0.70710678
    identity = jnp.eye(FEATURES, dtype=jnp.float32)
    return symmetric * (1.0 - identity) + diagonal_values[:, :, None] * identity


def draw_cross_old(key, part):
    subkeys = jax.random.split(jax.random.fold_in(key, 303), 2)
    diagonal_values = jax.random.uniform(subkeys[0], (LAYERS, FEATURES), jnp.float32, 0.2, 0.9)
    raw = jax.random.normal(subkeys[1], (LAYERS, FEATURES, FEATURES), jnp.float32)
    raw = raw * (0.3 / jnp.sqrt(jnp.float32(FEATURES)))
    identity = jnp.eye(FEATURES, dtype=jnp.float32)
    return raw * (1.0 - identity) + diagonal_values[:, :, None] * identity


def touch_ends(drawn, own_key, least, largest):
    spot = [jax.random.randint(jax.random.fold_in(own_key, axis), (), 0, length) for axis, length in enumerate(drawn.shape)]
    longest = drawn.shape.index(max(drawn.shape))
    beside = spot[:longest] + [(spot[longest] + 1) % drawn.shape[longest]] + spot[longest + 1:]
    return drawn.at[tuple(spot)].set(least).at[tuple(beside)].set(largest)


def block_levels(key, extent, cuts, low, largest):
    def one(dim, blocks):
        draws = jax.random.uniform(jax.random.fold_in(jax.random.fold_in(key, 6), dim), (blocks,), jnp.float32, low / len(cuts), largest / len(cuts))
        return jnp.repeat(jnp.exp(draws), extent[dim] // blocks).reshape((-1,) + (1,) * (len(extent) - dim - 1))

    gain = one(*cuts[0])
    for cut in cuts[1:]:
        gain = gain * one(*cut)
    return gain


def centred(stream_key, extent, deviation, most, shards=(), kind=jnp.bfloat16):
    values = deviation * jax.random.normal(stream_key, extent, jnp.float32)
    if shards:
        values = values * block_levels(stream_key, extent, shards, -0.22, 0.18)
    return jnp.clip(values, -most, most).astype(kind)


def setup_inputs(seed: int = 0) -> dict:
    arg_keys = jax.random.split(jax.random.key(seed), 8)
    activations = draw_activations(jax.random.fold_in(arg_keys[7], 71), 0)
    factor_old = draw_factor_old(jax.random.fold_in(arg_keys[7], 71), 0)
    cross_old = draw_cross_old(jax.random.fold_in(arg_keys[7], 71), 0)
    gradients = centred(arg_keys[3], (LAYERS, FEATURES, OUTPUTS), 1.0, 6.0, ((0, 8), (1, 4)))
    moments = centred(arg_keys[4], (LAYERS, FEATURES, OUTPUTS), 1.0, 6.0, ((0, 8), (1, 4)))
    exponents = touch_ends(jax.random.randint(arg_keys[5], (LAYERS, FEATURES // SCALE_BLOCK), -3, 3), jax.random.fold_in(arg_keys[5], 1), -3, 2).astype(jnp.int32)
    master = centred(arg_keys[6], (LAYERS, FEATURES, OUTPUTS), 1.0, 6.0, ((0, 8), (1, 4)), jnp.float32)
    return dict(activations=activations, factor_old=factor_old, cross_old=cross_old, gradients=gradients, moments=moments, exponents=exponents, master=master)


FACTOR_DECAY = 0.9
DAMPING = 0.5
MOMENTUM = 0.8
STEP_SIZE = 0.05


def chain_solve(target, pivots, coupling):
    coupling_ratio = coupling / pivots

    def forward_step(passed, slices):
        target_layer, pivot_layer, coupled = slices
        scaled = (target_layer - passed) / pivot_layer[:, None]
        return coupled[:, None] * scaled, scaled

    zero_block = jnp.zeros(target.shape[1:], jnp.float32)
    _, scaled_all = lax.scan(forward_step, zero_block, (target, pivots, coupling))

    def backward_step(nearer, slices):
        scaled, ratio_layer = slices
        solved = scaled - ratio_layer[:, None] * nearer
        return solved, solved

    _, solved_all = lax.scan(backward_step, zero_block, (scaled_all, coupling_ratio), reverse=True)
    return solved_all


def reference(activations, factor_old, cross_old, gradients, moments, exponents, master):
    fresh_weight = (1.0 - FACTOR_DECAY) / TOKENS
    next_acts = jnp.concatenate([activations[1:], jnp.zeros_like(activations[:1])], 0)

    def refresh(slices):
        own_layer, next_layer, factor_prev, cross_prev = slices
        batch_factor = jnp.dot(own_layer.T, own_layer, preferred_element_type=jnp.float32)
        batch_cross = jnp.dot(own_layer.T, next_layer, preferred_element_type=jnp.float32)
        return (FACTOR_DECAY * factor_prev + fresh_weight * batch_factor,
                FACTOR_DECAY * cross_prev + fresh_weight * batch_cross)

    factor_new, cross_new = lax.map(refresh, (activations, next_acts, factor_old, cross_old))
    diag_index = jnp.arange(FEATURES)
    pivots = DAMPING + factor_new[:, diag_index, diag_index]
    coupling = cross_new[:, diag_index, diag_index]
    grad_wide = gradients.astype(jnp.float32)
    initial = chain_solve(grad_wide, pivots, coupling).astype(jnp.bfloat16)
    initial_wide = initial.astype(jnp.float32)
    zero_sol = jnp.zeros_like(initial_wide[:1])
    upper_sol = jnp.concatenate([initial_wide[1:], zero_sol], 0)
    lower_sol = jnp.concatenate([zero_sol, initial_wide[:-1]], 0)
    cross_lower = jnp.concatenate([jnp.zeros_like(cross_new[:1]), cross_new[:-1]], 0)

    def apply_blocks(slices):
        factor_layer, cross_layer, cross_prev, own_block, upper_block, lower_block = slices
        result = jnp.dot(factor_layer, own_block, precision=lax.Precision.HIGHEST, preferred_element_type=jnp.float32)
        result = result + DAMPING * own_block
        result = result + jnp.dot(cross_layer, upper_block, precision=lax.Precision.HIGHEST, preferred_element_type=jnp.float32)
        result = result + jnp.dot(cross_prev.T, lower_block, precision=lax.Precision.HIGHEST, preferred_element_type=jnp.float32)
        return result

    applied = lax.map(apply_blocks, (factor_new, cross_new, cross_lower, initial_wide, upper_sol, lower_sol))
    update = initial_wide + chain_solve(grad_wide - applied, pivots, coupling)
    dequant = jnp.repeat(jnp.exp2(exponents.astype(jnp.float32)), SCALE_BLOCK, axis=1)[:, :, None]
    requant = jnp.repeat(jnp.exp2(-exponents.astype(jnp.float32)), SCALE_BLOCK, axis=1)[:, :, None]
    moment = MOMENTUM * moments.astype(jnp.float32) * dequant + (1.0 - MOMENTUM) * update
    moments_new = (moment * requant).astype(jnp.bfloat16)
    master_new = master - STEP_SIZE * moment
    replicas = master_new.astype(jnp.bfloat16)
    return factor_new, cross_new, moments_new, master_new, replicas
```

```python
import functools

import jax
import jax.numpy as jnp
from jax import lax
from jax.experimental import pallas as pl
from jax.experimental.pallas import tpu as pltpu
from jax.sharding import PartitionSpec as P

SCALE_BLOCK = 128


FACTOR_DECAY = 0.9
DAMPING = 0.5
MOMENTUM = 0.8
STEP_SIZE = 0.05


MESH = pl.DeviceIdType.MESH


def exchange_kernel(axis, count, modes, *refs):
    items = len(modes)
    sources, targets = refs[:items], refs[items : 2 * items]
    send_sem, recv_sem, local_sem = refs[2 * items :]
    mine = lax.axis_index(axis)
    barrier = pltpu.get_barrier_semaphore()
    for step in range(1, count):
        peer = lax.rem(mine + step, count)
        pl.semaphore_signal(barrier, inc=1, device_id={axis: peer}, device_id_type=MESH)
    pl.semaphore_wait(barrier, count - 1)
    remote, local = [], []
    for step in range(count - 1, 0, -1):
        peer = lax.rem(mine + step, count)
        for item, mode in enumerate(modes):
            if mode == "down" and step != count - 1:
                continue
            source = sources[item].at[peer] if mode == "swap" else sources[item]
            target = targets[item] if mode == "down" else targets[item].at[mine]
            remote.append(
                pltpu.make_async_remote_copy(
                    src_ref=source,
                    dst_ref=target,
                    send_sem=send_sem.at[item, step - 1],
                    recv_sem=recv_sem.at[item, step - 1],
                    device_id={axis: peer},
                    device_id_type=MESH,
                )
            )
            remote[-1].start()
    for item, mode in enumerate(modes):
        if mode != "down":
            source = sources[item].at[mine] if mode == "swap" else sources[item]
            local.append(
                pltpu.make_async_copy(source, targets[item].at[mine], local_sem.at[item])
            )
            local[-1].start()
    for copy in local + remote:
        copy.wait()


def exchange(axis, call_id, *pairs):
    count = lax.axis_size(axis)
    modes = tuple(mode for mode, _ in pairs)
    arrays = [array for _, array in pairs]
    shapes = [
        jax.ShapeDtypeStruct(
            (count,) + array.shape if mode == "gather" else array.shape, array.dtype
        )
        for mode, array in pairs
    ]
    sent = sum(array.size * array.dtype.itemsize for array in arrays)
    return pl.pallas_call(
        functools.partial(exchange_kernel, axis, count, modes),
        out_shape=shapes,
        in_specs=[pl.BlockSpec(memory_space=pltpu.VMEM)] * len(arrays),
        out_specs=[pl.BlockSpec(memory_space=pl.ANY)] * len(arrays),
        scratch_shapes=[
            pltpu.SemaphoreType.DMA((len(arrays), count - 1)),
            pltpu.SemaphoreType.DMA((len(arrays), count - 1)),
            pltpu.SemaphoreType.DMA((len(arrays),)),
        ],
        compiler_params=pltpu.CompilerParams(collective_id=call_id, has_side_effects=True),
        cost_estimate=pl.CostEstimate(flops=0, bytes_accessed=20 * sent, transcendentals=0),
        name=f"exchange_{call_id}",
    )(*arrays)


def solve_kernel(layers, with_lower, *refs):
    target_ref, refs = refs[0], refs[1:]
    if with_lower:
        lower_ref, refs = refs[0], refs[1:]
    pivot_ref, coupling_ref, out_ref, scaled_ref = refs
    passed = None
    for layer in range(layers):
        target = target_ref[layer].astype(jnp.float32)
        if layer:
            if with_lower:
                target = target - lower_ref[layer - 1].astype(jnp.float32)
            target = target - passed
        scaled = target / pivot_ref[layer]
        scaled_ref[layer] = scaled
        passed = coupling_ref[layer] * scaled
    solved = scaled
    out_ref[layers - 1] = solved.astype(out_ref.dtype)
    for layer in range(layers - 2, -1, -1):
        ratio = coupling_ref[layer] / pivot_ref[layer]
        solved = scaled_ref[layer] - ratio * solved
        out_ref[layer] = solved.astype(out_ref.dtype)


def chain_solve(target, pivots, coupling, lower=None):
    layers, rows, columns = target.shape
    width = 256 if columns % 256 == 0 else columns
    wide = pl.BlockSpec((layers, rows, width), lambda i: (0, 0, i))
    narrow = pl.BlockSpec((layers, rows, 1), lambda i: (0, 0, 0))
    arrays = (target,) if lower is None else (target, lower)
    return pl.pallas_call(
        functools.partial(solve_kernel, layers, lower is not None),
        out_shape=jax.ShapeDtypeStruct(target.shape, jnp.bfloat16),
        grid=(columns // width,),
        in_specs=[wide] * len(arrays) + [narrow] * 2,
        out_specs=wide,
        scratch_shapes=[pltpu.VMEM((layers, rows, width), jnp.float32)],
        cost_estimate=pl.CostEstimate(
            flops=10 * target.size, bytes_accessed=8 * target.size, transcendentals=0
        ),
        name="solve",
    )(*arrays, pivots, coupling)


def shifted(value, axis, steps):
    count = lax.axis_size(axis)
    leading, last = (max(0, -steps), min(count, count - steps))
    return lax.ppermute(value, axis, [(source, source + steps) for source in range(leading, last)])


def turned(value, axis, steps):
    count = lax.axis_size(axis)
    return lax.ppermute(value, axis, [(spot, (spot + steps) % count) for spot in range(count)])


def row_products(left_rows, right_rows):
    return lax.dot_general(
        left_rows, right_rows, (((0,), (0,)), ((), ())), preferred_element_type=jnp.float32
    )


def product(left, right):
    return jnp.dot(left, right, preferred_element_type=jnp.float32)


def halves(value):
    high = lax.reduce_precision(value, 8, 7)
    return high.astype(jnp.bfloat16), (value - high).astype(jnp.bfloat16)


def body(activations, factor_old, cross_old, gradients, moments, exponents, master):
    layers, groups = lax.axis_size("layer"), lax.axis_size("dp")
    layer, group = lax.axis_index("layer"), lax.axis_index("dp")
    own_acts = activations[0]
    row_count, features = factor_old.shape[1:]
    columns = gradients.shape[2]
    chunk = row_count // layers
    row_start = group * row_count
    fresh_weight = (1.0 - FACTOR_DECAY) / (activations.shape[1] * groups)

    all_tokens = lax.all_gather(own_acts, "dp", axis=0, tiled=True)
    cross_blocks = []
    for step in range(groups):
        place = lax.rem(group + step, groups) * row_count
        block = lax.dynamic_slice_in_dim(cross_old[0], place, row_count, 1).astype(jnp.bfloat16)
        cross_blocks.append(turned(block, "dp", step) if step else block)

    grad_swapped, next_acts = exchange(
        "layer",
        0,
        ("swap", gradients[0].reshape(layers, chunk, columns)),
        ("down", own_acts),
    )
    has_upper = (layer < layers - 1).astype(jnp.float32)
    own_wide, next_wide = own_acts.astype(jnp.float32), next_acts.astype(jnp.float32)
    sums = jnp.stack([jnp.sum(own_wide * own_wide, 0), has_upper * jnp.sum(own_wide * next_wide, 0)])
    sums = jnp.swapaxes(sums.reshape(2, groups, row_count), 0, 1)
    (sums,) = exchange("dp", 1, ("swap", sums))
    sums = jnp.sum(sums, 0)
    eye = jnp.eye(row_count, dtype=jnp.bool_)

    def diagonal(rows):
        square = lax.dynamic_slice_in_dim(rows, row_start, row_count, 1)
        return jnp.sum(jnp.where(eye, square, 0.0), 0)

    pivots = DAMPING + FACTOR_DECAY * diagonal(factor_old[0]) + fresh_weight * sums[0]
    coupling = FACTOR_DECAY * diagonal(cross_old[0]) + fresh_weight * sums[1]
    (scales,) = exchange("layer", 2, ("gather", jnp.stack([pivots, coupling])))
    scales = lax.dynamic_slice_in_dim(scales, layer * chunk, chunk, 2)
    pivots, coupling = scales[:, 0, :, None], scales[:, 1, :, None]

    initial = chain_solve(grad_swapped, pivots, coupling)
    (initial,) = exchange("layer", 3, ("swap", initial))
    initial = initial.reshape(row_count, columns)

    upper_acts = shifted(all_tokens, "layer", -1)
    own_columns = lax.dynamic_slice_in_dim(all_tokens, row_start, row_count, 1)
    upper_columns = lax.dynamic_slice_in_dim(upper_acts, row_start, row_count, 1)
    factor_new = FACTOR_DECAY * factor_old[0] + fresh_weight * row_products(own_columns, all_tokens)
    cross_new = FACTOR_DECAY * cross_old[0] + fresh_weight * row_products(own_columns, upper_acts)
    batch_turned = (fresh_weight * row_products(upper_columns, all_tokens)).astype(jnp.bfloat16)
    factor_high, factor_low = halves(factor_new)
    cross_high, cross_low = halves(cross_new)

    pieces = 2
    width = columns // pieces
    residual, lowered = [], []
    for piece in range(pieces):
        part = slice(piece * width, (piece + 1) * width)
        own_full = lax.all_gather(initial[:, part], "dp", axis=0, tiled=True)
        upper_full = shifted(own_full, "layer", -1)
        transposed = product(batch_turned, own_full)
        for step in range(groups):
            place = lax.rem(group - step + groups, groups) * row_count
            rows = lax.dynamic_slice_in_dim(own_full, place, row_count, 0)
            transposed = transposed + FACTOR_DECAY * row_products(cross_blocks[step], rows)
        lowered.append(transposed.astype(jnp.bfloat16))
        applied = product(factor_high, own_full) + product(factor_low, own_full)
        applied = applied + DAMPING * initial[:, part].astype(jnp.float32)
        applied = applied + product(cross_high, upper_full) + product(cross_low, upper_full)
        residual.append((gradients[0][:, part].astype(jnp.float32) - applied).astype(jnp.bfloat16))
    residual = jnp.concatenate(residual, 1).reshape(layers, chunk, columns)
    lowered = jnp.concatenate(lowered, 1).reshape(layers, chunk, columns)
    residual, lowered = exchange("layer", 4, ("swap", residual), ("swap", lowered))
    correction = chain_solve(residual, pivots, coupling, lowered)
    (correction,) = exchange("layer", 5, ("swap", correction))
    correction = correction.reshape(row_count, columns)

    update = initial.astype(jnp.float32) + correction.astype(jnp.float32)
    dequant = jnp.repeat(jnp.exp2(exponents[0].astype(jnp.float32)), SCALE_BLOCK)[:, None]
    requant = jnp.repeat(jnp.exp2(-exponents[0].astype(jnp.float32)), SCALE_BLOCK)[:, None]
    moment = MOMENTUM * moments[0].astype(jnp.float32) * dequant + (1.0 - MOMENTUM) * update
    moments_new = (moment * requant).astype(jnp.bfloat16)
    master_new = master[0] - STEP_SIZE * moment
    replicas = lax.all_gather(master_new.astype(jnp.bfloat16), "dp", axis=0, tiled=True)
    return (factor_new[None], cross_new[None], moments_new[None], master_new[None], replicas[None])


def solution(mesh):
    return jax.shard_map(
        body,
        mesh=mesh,
        in_specs=(
            P("layer", "dp", None),
            P("layer", "dp", None),
            P("layer", "dp", None),
            P("layer", "dp", None),
            P("layer", "dp", None),
            P("layer", "dp"),
            P("layer", "dp", None),
        ),
        out_specs=(
            P("layer", "dp", None),
            P("layer", "dp", None),
            P("layer", "dp", None),
            P("layer", "dp", None),
            P("layer", None, None),
        ),
        check_vma=False,
    )
```

```python
import functools

import jax
import jax.numpy as jnp
from jax import lax
from jax.experimental import pallas as pl
from jax.experimental.pallas import tpu as pltpu
from jax.sharding import PartitionSpec as P


SCALE_BLOCK = 128


FACTOR_DECAY = 0.9
DAMPING = 0.5
MOMENTUM = 0.8
STEP_SIZE = 0.05


MESH = pl.DeviceIdType.MESH


def exchange_kernel(axis, count, modes, *refs):
    items = len(modes)
    sources, targets = refs[:items], refs[items : 2 * items]
    send_sem, recv_sem, local_sem = refs[2 * items :]
    mine = lax.axis_index(axis)
    barrier = pltpu.get_barrier_semaphore()
    for step in range(1, count):
        peer = lax.rem(mine + step, count)
        pl.semaphore_signal(barrier, inc=1, device_id={axis: peer}, device_id_type=MESH)
    pl.semaphore_wait(barrier, count - 1)
    remote, local = [], []
    for step in range(count - 1, 0, -1):
        peer = lax.rem(mine + step, count)
        for item, mode in enumerate(modes):
            if mode == "down" and step != count - 1:
                continue
            source = sources[item].at[peer] if mode == "swap" else sources[item]
            target = targets[item] if mode == "down" else targets[item].at[mine]
            remote.append(
                pltpu.make_async_remote_copy(
                    src_ref=source,
                    dst_ref=target,
                    send_sem=send_sem.at[item, step - 1],
                    recv_sem=recv_sem.at[item, step - 1],
                    device_id={axis: peer},
                    device_id_type=MESH,
                )
            )
            remote[-1].start()
    for item, mode in enumerate(modes):
        if mode != "down":
            source = sources[item].at[mine] if mode == "swap" else sources[item]
            local.append(
                pltpu.make_async_copy(source, targets[item].at[mine], local_sem.at[item])
            )
            local[-1].start()
    for copy in local + remote:
        copy.wait()


def exchange(axis, call_id, *pairs):
    count = lax.axis_size(axis)
    modes = tuple(mode for mode, _ in pairs)
    arrays = [array for _, array in pairs]
    shapes = [
        jax.ShapeDtypeStruct(
            (count,) + array.shape if mode == "gather" else array.shape, array.dtype
        )
        for mode, array in pairs
    ]
    sent = sum(array.size * array.dtype.itemsize for array in arrays)
    return pl.pallas_call(
        functools.partial(exchange_kernel, axis, count, modes),
        out_shape=shapes,
        in_specs=[pl.BlockSpec(memory_space=pltpu.VMEM)] * len(arrays),
        out_specs=[pl.BlockSpec(memory_space=pl.ANY)] * len(arrays),
        scratch_shapes=[
            pltpu.SemaphoreType.DMA((len(arrays), count - 1)),
            pltpu.SemaphoreType.DMA((len(arrays), count - 1)),
            pltpu.SemaphoreType.DMA((len(arrays),)),
        ],
        compiler_params=pltpu.CompilerParams(collective_id=call_id, has_side_effects=True),
        cost_estimate=pl.CostEstimate(flops=0, bytes_accessed=20 * sent, transcendentals=0),
    )(*arrays)


def first_kernel(layers, target_ref, pivot_ref, coupling_ref, out_ref, scaled_ref):
    def target_of(layer):
        return target_ref[layer].astype(jnp.float32)

    sweep(layers, target_of, pivot_ref, coupling_ref, out_ref, scaled_ref)


def second_kernel(
    layers, target_ref, initial_ref, away_ref, lower_ref, pivot_ref, coupling_ref, out_ref, scaled_ref
):
    def target_of(layer):
        target = target_ref[layer].astype(jnp.float32)
        target = target - pivot_ref[layer] * initial_ref[layer].astype(jnp.float32)
        if layer < layers - 1:
            target = target - coupling_ref[layer] * initial_ref[layer + 1].astype(jnp.float32)
        target = target - away_ref[layer].astype(jnp.float32)
        if layer:
            target = target - coupling_ref[layer - 1] * initial_ref[layer - 1].astype(jnp.float32)
            target = target - lower_ref[layer - 1].astype(jnp.float32)
        return target

    sweep(layers, target_of, pivot_ref, coupling_ref, out_ref, scaled_ref)


def sweep(layers, target_of, pivot_ref, coupling_ref, out_ref, scaled_ref):
    passed = None
    for layer in range(layers):
        target = target_of(layer)
        if layer:
            target = target - passed
        scaled = target / pivot_ref[layer]
        scaled_ref[layer] = scaled
        passed = coupling_ref[layer] * scaled
    solved = scaled
    out_ref[layers - 1] = solved.astype(out_ref.dtype)
    for layer in range(layers - 2, -1, -1):
        ratio = coupling_ref[layer] / pivot_ref[layer]
        solved = scaled_ref[layer] - ratio * solved
        out_ref[layer] = solved.astype(out_ref.dtype)


def chain_solve(pivots, coupling, *arrays):
    layers, rows, columns = arrays[0].shape
    width = 256 if columns % 256 == 0 else columns
    wide = pl.BlockSpec((layers, rows, width), lambda i: (0, 0, i))
    narrow = pl.BlockSpec((layers, rows, 1), lambda i: (0, 0, 0))
    size = arrays[0].size
    return pl.pallas_call(
        functools.partial(first_kernel if len(arrays) == 1 else second_kernel, layers),
        out_shape=jax.ShapeDtypeStruct(arrays[0].shape, jnp.bfloat16),
        grid=(columns // width,),
        in_specs=[wide] * len(arrays) + [narrow] * 2,
        out_specs=wide,
        scratch_shapes=[pltpu.VMEM((layers, rows, width), jnp.float32)],
        cost_estimate=pl.CostEstimate(
            flops=10 * size, bytes_accessed=8 * size, transcendentals=0
        ),
        name="solve",
    )(*arrays, pivots, coupling)


def shifted(value, axis, steps):
    count = lax.axis_size(axis)
    leading, last = (max(0, -steps), min(count, count - steps))
    return lax.ppermute(value, axis, [(source, source + steps) for source in range(leading, last)])


def turned(value, axis, steps):
    count = lax.axis_size(axis)
    return lax.ppermute(value, axis, [(spot, (spot + steps) % count) for spot in range(count)])


def row_products(left_rows, right_rows):
    return lax.dot_general(
        left_rows, right_rows, (((0,), (0,)), ((), ())), preferred_element_type=jnp.float32
    )


def product(left, right):
    return jnp.dot(left, right, preferred_element_type=jnp.float32)


def halves(value):
    high = lax.reduce_precision(value, 8, 7)
    return high.astype(jnp.bfloat16), (value - high).astype(jnp.bfloat16)


def body(activations, factor_old, cross_old, gradients, moments, exponents, master):
    layers, groups = lax.axis_size("layer"), lax.axis_size("dp")
    layer, group = lax.axis_index("layer"), lax.axis_index("dp")
    own_acts = activations[0]
    row_count, _ = factor_old.shape[1:]
    columns = gradients.shape[2]
    chunk = row_count // layers
    row_start = group * row_count
    fresh_weight = (1.0 - FACTOR_DECAY) / (activations.shape[1] * groups)

    all_tokens = lax.all_gather(own_acts, "dp", axis=0, tiled=True)
    eye = jnp.eye(row_count, dtype=jnp.bool_)
    cross_blocks = []
    for step in range(groups):
        place = lax.rem(group + step, groups) * row_count
        block = lax.dynamic_slice_in_dim(cross_old[0], place, row_count, 1)
        if step:
            cross_blocks.append(turned(block.astype(jnp.bfloat16), "dp", step))
        else:
            cross_blocks.append(jnp.where(eye, 0.0, block).astype(jnp.bfloat16))

    grad_swapped, next_acts = exchange(
        "layer",
        0,
        ("swap", gradients[0].reshape(layers, chunk, columns)),
        ("down", own_acts),
    )
    has_upper = (layer < layers - 1).astype(jnp.float32)
    own_wide, next_wide = own_acts.astype(jnp.float32), next_acts.astype(jnp.float32)
    sums = jnp.stack([jnp.sum(own_wide * own_wide, 0), has_upper * jnp.sum(own_wide * next_wide, 0)])
    sums = jnp.swapaxes(sums.reshape(2, groups, row_count), 0, 1)
    (sums,) = exchange("dp", 1, ("swap", sums))
    sums = jnp.sum(sums, 0)

    def diagonal(rows):
        square = lax.dynamic_slice_in_dim(rows, row_start, row_count, 1)
        return jnp.sum(jnp.where(eye, square, 0.0), 0)

    own_diagonal = FACTOR_DECAY * diagonal(factor_old[0]) + fresh_weight * sums[0]
    own_coupling = FACTOR_DECAY * diagonal(cross_old[0]) + fresh_weight * sums[1]
    (scales,) = exchange("layer", 2, ("gather", jnp.stack([DAMPING + own_diagonal, own_coupling])))
    scales = lax.dynamic_slice_in_dim(scales, layer * chunk, chunk, 2)
    pivots, coupling = scales[:, 0, :, None], scales[:, 1, :, None]
    own_diagonal, own_coupling = own_diagonal[:, None], own_coupling[:, None]
    turned_diagonal = (fresh_weight * sums[1])[:, None]

    initial_swapped = chain_solve(pivots, coupling, grad_swapped)
    (initial,) = exchange("layer", 3, ("swap", initial_swapped))
    initial = initial.reshape(row_count, columns)

    pieces = 2
    width = columns // pieces
    parts = [slice(piece * width, (piece + 1) * width) for piece in range(pieces)]
    own_full = [lax.all_gather(initial[:, parts[0]], "dp", axis=0, tiled=True)]

    upper_acts = shifted(all_tokens, "layer", -1)
    own_columns = lax.dynamic_slice_in_dim(all_tokens, row_start, row_count, 1)
    upper_columns = lax.dynamic_slice_in_dim(upper_acts, row_start, row_count, 1)
    factor_new = FACTOR_DECAY * factor_old[0] + fresh_weight * row_products(own_columns, all_tokens)
    cross_new = FACTOR_DECAY * cross_old[0] + fresh_weight * row_products(own_columns, upper_acts)
    batch_turned = (fresh_weight * row_products(upper_columns, all_tokens)).astype(jnp.bfloat16)
    factor_high, factor_low = halves(factor_new)
    cross_high, cross_low = halves(cross_new)

    later = [initial[:, part] for part in parts[1:]]
    later, factor_high = lax.optimization_barrier((later, factor_high))
    own_full += [lax.all_gather(value, "dp", axis=0, tiled=True) for value in later]

    def leave(piece):
        full, near = own_full[piece], initial[:, parts[piece]].astype(jnp.float32)
        upper = shifted(full, "layer", -1)
        transposed = product(batch_turned, full)
        for step in range(groups):
            place = lax.rem(group - step + groups, groups) * row_count
            rows = lax.dynamic_slice_in_dim(full, place, row_count, 0)
            transposed = transposed + FACTOR_DECAY * row_products(cross_blocks[step], rows)
        transposed = (transposed - turned_diagonal * near).astype(jnp.bfloat16)
        away = product(factor_high, full) + product(factor_low, full) - own_diagonal * near
        upper_rows = lax.dynamic_slice_in_dim(upper, row_start, row_count, 0)
        away = away + product(cross_high, upper) + product(cross_low, upper)
        away = (away - own_coupling * upper_rows.astype(jnp.float32)).astype(jnp.bfloat16)
        return [value.reshape(layers, chunk, width) for value in (away, transposed)]

    dequant = jnp.repeat(jnp.exp2(exponents[0].astype(jnp.float32)), SCALE_BLOCK)[:, None]
    requant = jnp.repeat(jnp.exp2(-exponents[0].astype(jnp.float32)), SCALE_BLOCK)[:, None]
    results, sent = [], None
    for piece, part in enumerate(parts):
        away, lowered = leave(piece)
        if piece:
            gathered = lax.all_gather(sent, "dp", axis=0, tiled=True)
            away, lowered, held = lax.optimization_barrier((away, lowered, results[-1]))
            results[-1] = held + (gathered,)
        away, lowered = exchange("layer", 4 + 2 * piece, ("swap", away), ("swap", lowered))
        if piece + 1 < pieces:
            away, lowered, own_full[piece + 1] = lax.optimization_barrier(
                (away, lowered, own_full[piece + 1])
            )
        correction = chain_solve(
            pivots, coupling, grad_swapped[:, :, part], initial_swapped[:, :, part], away, lowered
        )
        (correction,) = exchange("layer", 5 + 2 * piece, ("swap", correction))
        correction = correction.reshape(row_count, width)
        update = initial[:, part].astype(jnp.float32) + correction.astype(jnp.float32)
        moment = MOMENTUM * moments[0][:, part].astype(jnp.float32) * dequant
        moment = moment + (1.0 - MOMENTUM) * update
        fresh_moments = (moment * requant).astype(jnp.bfloat16)
        fresh_master = master[0][:, part] - STEP_SIZE * moment
        sent = fresh_master.astype(jnp.bfloat16)
        results.append((fresh_moments, fresh_master))
    results[-1] += (lax.all_gather(sent, "dp", axis=0, tiled=True),)
    moments_new, master_new, replicas = [jnp.concatenate(values, 1) for values in zip(*results)]
    return (factor_new[None], cross_new[None], moments_new[None], master_new[None], replicas[None])


def solution(mesh):
    return jax.shard_map(
        body,
        mesh=mesh,
        in_specs=(
            P("layer", "dp", None),
            P("layer", "dp", None),
            P("layer", "dp", None),
            P("layer", "dp", None),
            P("layer", "dp", None),
            P("layer", "dp"),
            P("layer", "dp", None),
        ),
        out_specs=(
            P("layer", "dp", None),
            P("layer", "dp", None),
            P("layer", "dp", None),
            P("layer", "dp", None),
            P("layer", None, None),
        ),
        check_vma=False,
    )
```
